256 devices in a mesh: shard: 64 (over y, z, core), tensor: 4 (over x).
Axes of the slice: x: 4, y: 4, z: 8, core: 2. Of those that a mesh axis runs over, the one named last changes fastest.
Arguments:
- gradient: bfloat16 [64, 1024, 1024], P(None, 'shard', 'tensor'), may hold values from -64 to 64, as said below
- momentum: float32 [64, 1024, 1024], P(None, 'shard', 'tensor'), may hold values from -64 to 64, as said below
Outputs:
- momentum_out: float32 [64, 1024, 1024], P(None, 'shard', 'tensor')
- update: float32 [64, 1024, 1024], P(None, 'shard', 'tensor')
The draws below stay inside these ranges and needn't reach their ends.
Inputs may be any that keep to these rules, and one draw needn't show every extreme that they name: `gradient`: finite real values. `momentum`: finite real values.
All inputs are finite; a program needn't handle non-finite values.
Results may differ from the reference program's by a relative error of at most 0.0003.
Values sent between devices are 32-bit elements; how exact they have to be, the bound alone decides.
No kernel may reach another device: no remote copies, remote signals or barrier semaphores. Data moves between devices by JAX's collectives and lax.ppermute only.
A program may use at most 64 MiB of HBM per device.

```python
import math
import jax
import jax.numpy as jnp
from jax import lax

D = 1024
BLOCK = 1024
ITERS = 3
NB = 64


def scaled_field(key):
    noise_key, rows_key, column_key = jax.random.split(key, 3)
    row_scale = jnp.exp(jax.random.uniform(rows_key, (NB, BLOCK, 1), jnp.float32, 0.0, math.log(10.0)))
    column_scale = jnp.exp(jax.random.uniform(column_key, (NB, 1, D), jnp.float32, 0.0, math.log(10.0)))
    field_values = jnp.clip(jax.random.normal(noise_key, (NB, BLOCK, D), jnp.float32), -6.0, 6.0)
    return field_values * row_scale * column_scale / 10.0


def draw_gradient(key, part):
    return scaled_field(key).astype(jnp.bfloat16)


def draw_momentum(key, part):
    return scaled_field(jax.random.fold_in(key, 7)).astype(jnp.float32)


def setup_inputs(seed: int = 0) -> dict:
    keys = jax.random.split(jax.random.key(seed), 3)
    return {
        "gradient": draw_gradient(jax.random.fold_in(keys[2], 71), 0),
        "momentum": draw_momentum(jax.random.fold_in(keys[2], 71), 0),
    }


first_coef = 3.4445
second_coef = -4.775
third_coef = 2.0315
decay_rate = 0.95

def orthogonalize(matrix):
    frobenius = jnp.sqrt(jnp.sum(matrix * matrix)) + 1e-07
    iterate = matrix / frobenius
    for sweep_index in range(ITERS):
        gram_matrix = jnp.einsum('ij,lj->il', iterate, iterate, precision=lax.Precision.HIGHEST, preferred_element_type=jnp.float32)
        square = jnp.einsum('ij,jl->il', gram_matrix, gram_matrix, precision=lax.Precision.HIGHEST, preferred_element_type=jnp.float32)
        polynomial = second_coef * gram_matrix + third_coef * square
        iterate = first_coef * iterate + jnp.einsum('ij,jl->il', polynomial, iterate, precision=lax.Precision.HIGHEST, preferred_element_type=jnp.float32)
    return 0.2 * math.sqrt(max(BLOCK, D)) * iterate

def reference(gradient, momentum):
    widened = gradient.astype(jnp.float32)
    momentum_out = decay_rate * momentum + widened
    direction = widened + decay_rate * momentum_out
    update = lax.map(orthogonalize, direction)
    return (momentum_out, update)
```

```python
import functools
import math

import jax
import jax.numpy as jnp
from jax import lax
from jax.experimental import pallas as pl
from jax.experimental.pallas import tpu as pltpu
from jax.sharding import PartitionSpec as P

D = 1024
BLOCK = 1024
ITERS = 3
HALF = 512
TILE = 256

first_coef = 3.4445
second_coef = -4.775
third_coef = 2.0315
decay_rate = 0.95
out_scale = 0.2 * math.sqrt(max(BLOCK, D))

BY_ROWS = (((1,), (1,)), ((), ()))
BY_COLUMNS = (((1,), (0,)), ((), ()))

HOLDER = (
    ((0, 0, 0), (0, 1, 0), (1, 0, 0), (0, 1, 1)),
    ((0, 0, 1), (1, 1, 1), (1, 0, 1), (1, 1, 0)),
)
SIDE_TO_HOME = (((1, 0), (0, 0)), ((3, 0), (0, 1)), ((3, 1), (2, 0)), ((1, 1), (2, 1)))


def momentum_kernel(gradient_ref, momentum_ref, momentum_out_ref, send_ref):
    widened = gradient_ref[...].astype(jnp.float32)
    momentum_out = decay_rate * momentum_ref[...] + widened
    momentum_out_ref[...] = momentum_out
    direction = widened + decay_rate * momentum_out
    for line in range(direction.shape[0] // 2):
        for core in range(2):
            for tensor in range(4):
                which, rh, ch = HOLDER[core][tensor]
                send_ref[line * 8 + core * 4 + tensor] = direction[
                    line * 2 + which, rh * 8 : rh * 8 + 8, ch * 128 : ch * 128 + 128
                ]


def place_kernel(tiles_ref, update_ref):
    for line in range(update_ref.shape[0] // 2):
        for core in range(2):
            for tensor in range(4):
                which, rh, ch = HOLDER[core][tensor]
                update_ref[line * 2 + which, rh * 8 : rh * 8 + 8, ch * 128 : ch * 128 + 128] = tiles_ref[
                    line * 8 + core * 4 + tensor
                ]


def split(value):
    high = value.astype(jnp.bfloat16)
    return high, (value - high.astype(jnp.float32)).astype(jnp.bfloat16)


def product(left, right, dims):
    dot = functools.partial(lax.dot_general, dimension_numbers=dims, preferred_element_type=jnp.float32)
    return dot(left[0], right[0]) + (dot(left[0], right[1]) + dot(left[1], right[0]))


def rows(index):
    return pl.ds(pl.multiple_of(index * TILE, TILE), TILE)


def newton_schulz_kernel(own_top, own_bottom, other_top, other_bottom, out_top, out_bottom, *scratch):
    first, second, gram, poly = (scratch[i : i + 2] for i in (0, 2, 4, 6))
    count = BLOCK // TILE

    squares = jnp.float32(0)
    for r, c, piece in ((0, 0, own_top), (HALF, 0, own_bottom), (0, HALF, other_top), (HALF, HALF, other_bottom)):

        def load(index, total, r=r, c=c, piece=piece):
            value = piece[rows(index), :]
            high, low = split(value)
            place = pl.ds(pl.multiple_of(r + index * TILE, TILE), TILE)
            first[0][place, c : c + HALF] = high
            first[1][place, c : c + HALF] = low
            return total + jnp.sum(value * value)

        squares = lax.fori_loop(0, HALF // TILE, load, squares)
    inverse = 1.0 / (jnp.sqrt(squares) + 1e-07)

    def symmetric(source, target, finish):
        def outer(i, carry):
            def inner(j, carry):
                left = tuple(part[rows(i), :] for part in source)
                right = tuple(part[rows(j), :] for part in source)
                value = finish(product(left, right, BY_ROWS), i, j)
                target[0][rows(i), rows(j)], target[1][rows(i), rows(j)] = split(value)

                @pl.when(i != j)
                def _():
                    target[0][rows(j), rows(i)], target[1][rows(j), rows(i)] = split(value.T)

                return carry

            return lax.fori_loop(0, i + 1, inner, carry)

        lax.fori_loop(0, count, outer, 0)

    for sweep_index in range(ITERS):
        source, target = ((first, second), (second, first))[sweep_index % 2]
        last = sweep_index == ITERS - 1
        scale = inverse if sweep_index == 0 else jnp.float32(1)
        symmetric(source, gram, lambda value, i, j: value * (scale * scale))

        def polynomial(value, i, j):
            gram_tile = gram[0][rows(i), rows(j)].astype(jnp.float32) + gram[1][rows(i), rows(j)].astype(jnp.float32)
            row = lax.broadcasted_iota(jnp.int32, value.shape, 0)
            column = lax.broadcasted_iota(jnp.int32, value.shape, 1)
            diagonal = jnp.where((row == column) & (i == j), jnp.float32(first_coef), jnp.float32(0))
            return (diagonal + (second_coef * gram_tile + third_coef * value)) * scale

        symmetric(gram, poly, polynomial)

        def apply(i, carry):
            left = tuple(part[rows(i), :] for part in poly)

            def inner(j, carry):
                right = tuple(part[:, rows(j)] for part in source)
                value = product(left, right, BY_COLUMNS)
                if not last:
                    target[0][rows(i), rows(j)], target[1][rows(i), rows(j)] = split(value)
                else:

                    @pl.when(i < count // 2)
                    def _():
                        out_top[rows(i), rows(j)] = out_scale * value

                    @pl.when(i >= count // 2)
                    def _():
                        out_bottom[rows(i - count // 2), rows(j)] = out_scale * value

                return carry

            return lax.fori_loop(0, HALF // TILE if last else count, inner, carry)

        lax.fori_loop(0, count, apply, 0)


def newton_schulz(*pieces):
    in_vmem = pl.BlockSpec(memory_space=pltpu.VMEM)
    return pl.pallas_call(
        newton_schulz_kernel,
        out_shape=[jax.ShapeDtypeStruct((HALF, HALF), jnp.float32)] * 2,
        in_specs=[in_vmem] * 4,
        out_specs=[in_vmem] * 2,
        scratch_shapes=[pltpu.VMEM((BLOCK, BLOCK), jnp.bfloat16)] * 8,
        compiler_params=pltpu.CompilerParams(vmem_limit_bytes=40 * 1024 * 1024),
        name="newton_schulz",
    )(*pieces)


def from_tiles(tiles):
    return tiles.reshape(64, 4, 8, 128).transpose(0, 2, 1, 3).reshape(HALF, HALF)


def to_tiles(quarter):
    return quarter.reshape(64, 8, 4, 128).transpose(0, 2, 1, 3).reshape(256, 8, 128)


def per_device(gradient, momentum):
    axes = ("shard", "tensor")
    lines = 32

    def device(p, place):
        tensor, core = place
        return (2 * p + core) * 4 + tensor

    inward = [(device(p, side), device(p, home)) for p in range(lines) for side, home in SIDE_TO_HOME]
    outward = [(home, side) for side, home in inward]
    swap = [(device(p, (t, c)), device(p, (t, 1 - c))) for p in range(lines) for t in (0, 2) for c in (0, 1)]

    step = 8
    blocked = pl.BlockSpec((step, 16, 256), lambda i: (i, 0, 0))
    tiled = pl.BlockSpec((step * 4, 8, 128), lambda i: (i, 0, 0))
    momentum_out, send = pl.pallas_call(
        momentum_kernel,
        grid=(64 // step,),
        out_shape=[
            jax.ShapeDtypeStruct((64, 16, 256), jnp.float32),
            jax.ShapeDtypeStruct((256, 8, 128), jnp.float32),
        ],
        in_specs=[blocked, blocked],
        out_specs=[blocked, tiled],
        name="momentum",
    )(gradient, momentum)

    own_top = from_tiles(lax.all_to_all(send, axes, split_axis=0, concat_axis=0, tiled=True))
    own_bottom = lax.ppermute(own_top, axes, inward)
    other_top = lax.ppermute(own_top, axes, swap)
    other_bottom = lax.ppermute(own_bottom, axes, swap)
    out_top, out_bottom = newton_schulz(own_top, own_bottom, other_top, other_bottom)
    is_home = (lax.axis_index("tensor") & 1) == 0
    result = jnp.where(is_home, out_top, lax.ppermute(out_bottom, axes, outward))
    tiles = lax.all_to_all(to_tiles(result), axes, split_axis=0, concat_axis=0, tiled=True)
    update = pl.pallas_call(
        place_kernel,
        grid=(64 // step,),
        out_shape=jax.ShapeDtypeStruct((64, 16, 256), jnp.float32),
        in_specs=[tiled],
        out_specs=blocked,
        name="place",
    )(tiles)
    return (momentum_out, update)


def solution(mesh):
    placed = (P(None, "shard", "tensor"), P(None, "shard", "tensor"))
    return jax.shard_map(
        per_device,
        mesh=mesh,
        in_specs=placed,
        out_specs=placed,
        check_vma=False,
    )
```

```python
import math

import jax
import jax.numpy as jnp
from jax import lax
from jax.experimental import pallas as pl
from jax.experimental.pallas import tpu as pltpu
from jax.sharding import PartitionSpec as P

D = 1024
BLOCK = 1024
ITERS = 3
HALF = 512
TILE = 256

first_coef = 3.4445
second_coef = -4.775
third_coef = 2.0315
decay_rate = 0.95
out_scale = 0.2 * math.sqrt(max(BLOCK, D))

PIECE_ROWS = (512, 176, 176, 160)
PIECE_STARTS = (0, 512, 688, 864)

BY_ROWS = (((1,), (1,)), ((), ()))
BY_COLUMNS = (((1,), (0,)), ((), ()))

SIZES = (4, 4, 8)
LINES = (22, 22, 20)
STARTS = (0, 22, 44)
CHIPS = [(x, y, z) for y in range(4) for z in range(8) for x in range(4)]
HOMES = [chip for chip in CHIPS if sum(chip) % 2 == 0]


def device(chip, core):
    x, y, z = chip
    return ((y * 8 + z) * 2 + core) * 4 + x


def neighbour(chip, axis, step):
    return tuple((c + step) % SIZES[i] if i == axis else c for i, c in enumerate(chip))


def side(chip, core, axis):
    return device(neighbour(chip, axis, 1 if core else -1), core)


def lower_holder(chip, core):
    line = lax.axis_index("shard")
    x, y, z = (side(chip, core, axis) for axis in range(3))
    return jnp.where(line < STARTS[1], x, jnp.where(line < STARTS[2], y, z))


def direction_kernel(gradient_ref, momentum_ref, send_ref):
    for block, chip in enumerate(HOMES):
        widened = gradient_ref[block].astype(jnp.float32)
        direction = widened + decay_rate * (decay_rate * momentum_ref[block] + widened)
        for core in range(2):
            columns = slice(core * 128, core * 128 + 128)
            send_ref[device(chip, core)] = direction[:8, columns]
            send_ref[lower_holder(chip, core)] = direction[8:, columns]


def place_kernel(tiles_ref, update_ref):
    for block, chip in enumerate(HOMES):
        for core in range(2):
            columns = slice(core * 128, core * 128 + 128)
            update_ref[block, :8, columns] = tiles_ref[device(chip, core)]
            update_ref[block, 8:, columns] = tiles_ref[lower_holder(chip, core)]


def split(value):
    high = value.astype(jnp.bfloat16)
    return high, (value - high.astype(jnp.float32)).astype(jnp.bfloat16)


def dot(left, right, dims):
    return lax.dot_general(left, right, dims, preferred_element_type=jnp.float32)


def product(left, right, dims):
    return dot(left[0], right[0], dims) + (dot(left[0], right[1], dims) + dot(left[1], right[0], dims))


def newton_schulz_kernel(*refs):
    pieces, outs, scratch = refs[:4], refs[4:8], refs[8:]
    iterate, gram, poly = (scratch[i : i + 2] for i in (0, 2, 4))
    panels = [slice(i, i + TILE) for i in range(0, BLOCK, TILE)]

    squares = jnp.zeros((16, HALF), jnp.float32)
    for index, piece in enumerate(pieces):
        base, c = (index % 2) * HALF, (index // 2) * HALF
        for r in range(0, HALF, 16):
            value = piece[r : r + 16, :]
            place = slice(base + r, base + r + 16)
            iterate[0][0, place, c : c + HALF], iterate[1][0, place, c : c + HALF] = split(value)
            squares = squares + value * value
    inverse = 1.0 / (jnp.sqrt(jnp.sum(squares)) + 1e-07)

    def symmetric(source, target, finish):
        for i, panel in enumerate(panels):
            high, low = (part[panel, :] for part in source)
            cross = dot(high, low, BY_ROWS)
            value = finish(dot(high, high, BY_ROWS) + (cross + cross.T), panel, panel)
            target[0][panel, panel], target[1][panel, panel] = split(value)
            if i:
                before = slice(0, i * TILE)
                value = finish(product((high, low), tuple(part[before, :] for part in source), BY_ROWS), panel, before)
                target[0][panel, before], target[1][panel, before] = split(value)
                target[0][before, panel], target[1][before, panel] = split(value.T)

    def sweep(sweep_index, carry):
        now = sweep_index & 1
        source = tuple(part.at[now] for part in iterate)
        target = tuple(part.at[1 - now] for part in iterate)
        scale = jnp.where(sweep_index == 0, inverse, jnp.float32(1))
        symmetric(source, gram, lambda value, panel, columns: value * (scale * scale))

        def polynomial(value, panel, columns):
            gram_tile = gram[0][panel, columns].astype(jnp.float32) + gram[1][panel, columns].astype(jnp.float32)
            value = (second_coef * scale) * gram_tile + (third_coef * scale) * value
            if panel == columns:
                row = lax.broadcasted_iota(jnp.int32, value.shape, 0)
                column = lax.broadcasted_iota(jnp.int32, value.shape, 1)
                value = value + jnp.where(row == column, first_coef * scale, jnp.float32(0))
            return value

        symmetric(gram, poly, polynomial)

        def apply(half, carry):
            columns = pl.ds(pl.multiple_of(half * HALF, HALF), HALF)
            right = tuple(part[:, columns] for part in source)
            for panel in panels:
                value = product(tuple(part[panel, :] for part in poly), right, BY_COLUMNS)
                target[0][panel, columns], target[1][panel, columns] = split(value)
                for start, out in zip(PIECE_STARTS, outs):
                    low = max(start, panel.start)
                    high = min(start + out.shape[0], panel.stop)
                    if low < high:
                        out[low - start : high - start, :] = out_scale * value[low - panel.start : high - panel.start]
            return carry

        return lax.fori_loop(0, jnp.where(sweep_index == ITERS - 1, 1, 2), apply, carry)

    lax.fori_loop(0, ITERS, sweep, 0)


def newton_schulz(*pieces):
    in_vmem = pl.BlockSpec(memory_space=pltpu.VMEM)
    return pl.pallas_call(
        newton_schulz_kernel,
        out_shape=[jax.ShapeDtypeStruct((n, HALF), jnp.float32) for n in PIECE_ROWS],
        in_specs=[in_vmem] * 4,
        out_specs=[in_vmem] * 4,
        scratch_shapes=[pltpu.VMEM((2, BLOCK, BLOCK), jnp.bfloat16)] * 2 + [pltpu.VMEM((BLOCK, BLOCK), jnp.bfloat16)] * 4,
        compiler_params=pltpu.CompilerParams(vmem_limit_bytes=40 * 1024 * 1024),
        name="newton_schulz",
    )(*pieces)


def from_tiles(tiles):
    return tiles.reshape(64, 4, 8, 128).transpose(0, 2, 1, 3).reshape(HALF, HALF)


def to_tiles(quarter):
    return quarter.reshape(64, 8, 4, 128).transpose(0, 2, 1, 3).reshape(256, 8, 128)


def per_device(gradient, momentum):
    axes = ("shard", "tensor")
    cores = (0, 1)
    inward = [[(side(chip, core, axis), device(chip, core)) for chip in HOMES for core in cores] for axis in range(3)]
    swap = [(device(chip, core), device(chip, 1 - core)) for chip in HOMES for core in cores]

    whole = pl.BlockSpec(memory_space=pltpu.VMEM)
    small = pltpu.CompilerParams(vmem_limit_bytes=16 * 1024 * 1024)
    send = pl.pallas_call(
        direction_kernel,
        out_shape=jax.ShapeDtypeStruct((256, 8, 128), jnp.float32),
        in_specs=[whole] * 2,
        out_specs=whole,
        compiler_params=small,
        name="direction",
    )(gradient, momentum)
    momentum_out = decay_rate * momentum + gradient.astype(jnp.float32)

    received = from_tiles(lax.all_to_all(send, axes, split_axis=0, concat_axis=0, tiled=True))
    arrived = []
    for pairs, start, count in zip(inward, STARTS, LINES):
        arrived.append(lax.ppermute(received[start * 8 : (start + count) * 8], axes, pairs))
    own = (received, jnp.concatenate(arrived, axis=0))
    other = [lax.ppermute(piece, axes, swap) for piece in own]
    top, *bottom = newton_schulz(*own, *other)
    outward = [[(home, holder) for holder, home in pairs] for pairs in inward]
    passed = jnp.concatenate([lax.ppermute(piece, axes, pairs) for piece, pairs in zip(bottom, outward)], axis=0)
    line = lax.axis_index("shard") >> 1
    is_home = ((lax.axis_index("tensor") + (line >> 3) + line) & 1) == 0
    result = jnp.where(is_home, top, passed)
    tiles = lax.all_to_all(to_tiles(result), axes, split_axis=0, concat_axis=0, tiled=True)
    update = pl.pallas_call(
        place_kernel,
        out_shape=jax.ShapeDtypeStruct((64, 16, 256), jnp.float32),
        in_specs=[whole],
        out_specs=whole,
        compiler_params=small,
        name="place",
    )(tiles)
    return (momentum_out, update)


def solution(mesh):
    placed = (P(None, "shard", "tensor"), P(None, "shard", "tensor"))
    return jax.shard_map(
        per_device,
        mesh=mesh,
        in_specs=placed,
        out_specs=placed,
        check_vma=False,
    )
```
